32 devices in a mesh: dp: 4 (over z), tensor: 4 (over y, x), section: 2 (over core).
Axes of the slice: x: 2, y: 2, z: 4, core: 2. Of those that a mesh axis runs over, the one named last changes fastest.
Arguments:
- grads: bfloat16 [4, 2, 768, 768], P('dp', 'section', 'tensor'), may hold values from -6 to 6
- errors: float32 [4, 2, 768, 768], P('dp', 'section', 'tensor'), may hold values from -3 to 3
- q_prev: float32 [2, 768, 32], P('section'), may hold values from -0.21875 to 0.21875
- p_root: float32 [2, 32, 32], P('section')
- q_root: float32 [2, 32, 32], P('section')
- momentum: float32 [2, 768, 768], P('section', 'tensor')
- weights: float32 [2, 768, 768], P('section', 'tensor'), may hold values from -0.21875 to 0.21875
- vec_grads: float32 [4, 2, 3, 768], P('dp', 'section', None, 'tensor'), may hold values from -6 to 6
- vec_momentum: float32 [2, 3, 768], P('section', None, 'tensor'), may hold values from -6 to 6
- vec_params: float32 [2, 3, 768], P('section', None, 'tensor'), may hold values from -3 to 3
Outputs:
- errors_out: float32 [4, 2, 768, 768], P('dp', 'section', 'tensor')
- p_factor: float32 [2, 768, 32], P('section', 'tensor')
- q_factor: float32 [2, 768, 32], P('section')
- momentum_out: float32 [2, 768, 768], P('section', 'tensor')
- weights_out: float32 [2, 768, 768], P('section', 'tensor')
- vec_momentum_out: float32 [2, 3, 768], P('section', None, 'tensor')
- vec_params_out: float32 [2, 3, 768], P('section', None, 'tensor')
The draws below stay inside these ranges and needn't reach their ends.
All inputs are finite; a program needn't handle non-finite values.
Results may differ from the reference program's by a relative error of at most 0.0003.
Values sent between devices are 32-bit elements; how exact they have to be, the bound alone decides.
A program may use at most 64 MiB of HBM per device.

```python
import math
import jax
import jax.numpy as jnp
from jax import lax

D = 768
R = 32
REPLICAS = 4
TENSOR_WAYS = 4


def make_root(key, factor):
    key_diag, key_off = jax.random.split(key)
    diag_part = jax.random.uniform(key_diag, (2, R, R), jnp.float32, 1.0, 2.0)
    off_part = jnp.clip(0.1 * jax.random.normal(key_off, (2, R, R), jnp.float32), -0.4, 0.4)
    eye_mask = jnp.eye(R, dtype=jnp.float32)[None]
    return (eye_mask * diag_part + (1.0 - eye_mask) * off_part) * factor


def draw_p_root(key, part):
    return make_root(jax.random.fold_in(key, 11), 1.0 / math.sqrt(REPLICAS))


def draw_q_root(key, part):
    return make_root(jax.random.fold_in(key, 23), 2.0 / math.sqrt(REPLICAS * D))


def draw_momentum(key, part):
    key = jax.random.fold_in(key, 37)
    key_base, key_rows, key_cols = jax.random.split(key, 3)
    rows_factor = jnp.exp(jax.random.uniform(key_rows, (2, D, 1), jnp.float32) * math.log(10.0))
    cols_factor = jnp.exp(jax.random.uniform(key_cols, (2, 1, D), jnp.float32) * math.log(10.0))
    row_index = jnp.arange(D, dtype=jnp.int32)[None, :, None]
    section_index = jnp.arange(2, dtype=jnp.int32)[:, None, None]
    position = (2 * (row_index // (D // TENSOR_WAYS)) + section_index).astype(jnp.float32)
    base = jnp.clip(jax.random.normal(key_base, (2, D, D), jnp.float32), -6.0, 6.0)
    trend = jnp.exp(math.log(3.0) * position / (2 * TENSOR_WAYS - 1))
    return 0.1 * base * rows_factor * cols_factor * trend


def steps_of(own_key, dims, cuts, smallest, largest):
    level = 1.0
    for dim, blocks in cuts:
        steps = jax.random.uniform(jax.random.fold_in(jax.random.fold_in(own_key, 6), dim), (blocks,), jnp.float32, smallest / len(cuts), largest / len(cuts))
        level = level * jnp.repeat(jnp.exp(steps), dims[dim] // blocks).reshape((-1,) + (1,) * (len(dims) - 1 - dim))
    return level


def scatter_about(stream_key, shape, width, bound, cuts=(), kind=jnp.bfloat16):
    array = width * jax.random.normal(stream_key, shape, jnp.float32)
    if cuts:
        array = array * steps_of(stream_key, shape, cuts, -0.22, 0.18)
    return jnp.clip(array, -bound, bound).astype(kind)


def setup_inputs(seed: int = 0) -> dict:
    key_list = jax.random.split(jax.random.key(seed), 11)
    return {
        "grads": scatter_about(key_list[0], (REPLICAS, 2, D, D), 1.0, 6.0, ((0, 4), (1, 2), (2, 4))),
        "errors": scatter_about(key_list[1], (REPLICAS, 2, D, D), 0.5, 3.0, ((0, 4), (1, 2), (2, 4)), jnp.float32),
        "q_prev": scatter_about(key_list[2], (2, D, R), D ** -0.5, 0.21875, ((0, 2),), jnp.float32),
        "p_root": draw_p_root(jax.random.fold_in(key_list[10], 71), 0),
        "q_root": draw_q_root(jax.random.fold_in(key_list[10], 71), 0),
        "momentum": draw_momentum(jax.random.fold_in(key_list[10], 71), 0),
        "weights": scatter_about(key_list[6], (2, D, D), D ** -0.5, 0.21875, ((0, 2), (1, 4)), jnp.float32),
        "vec_grads": scatter_about(key_list[7], (REPLICAS, 2, 3, D), 1.0, 6.0, ((0, 4), (1, 2), (3, 4)), jnp.float32),
        "vec_momentum": scatter_about(key_list[8], (2, 3, D), 1.0, 6.0, ((0, 2), (2, 4)), jnp.float32),
        "vec_params": scatter_about(key_list[9], (2, 3, D), 0.5, 3.0, ((0, 2), (2, 4)), jnp.float32),
    }


HIGH = lax.Precision.HIGHEST

def reference(grads, errors, q_prev, p_root, q_root, momentum, weights, vec_grads, vec_momentum, vec_params):
    merged = grads.astype(jnp.float32) + errors
    p_sum = jnp.einsum('nsdc,sck->sdk', merged, q_prev, precision=HIGH)
    p_factor = jnp.einsum('sdk,skj->sdj', p_sum, p_root, precision=HIGH)
    q_sum = jnp.einsum('nsdc,sdk->sck', merged, p_factor, precision=HIGH)
    q_factor = jnp.einsum('sck,skj->scj', q_sum, q_root, precision=HIGH)
    approx = jnp.einsum('sdk,sck->sdc', p_factor, q_factor, precision=HIGH) / REPLICAS
    errors_out = merged - approx[None]
    vec_mean = lax.optimization_barrier(jnp.sum(vec_grads, axis=0)) / REPLICAS
    momentum_out = 0.9 * momentum + approx
    vec_momentum_out = 0.9 * vec_momentum + vec_mean
    total = jnp.sum(momentum_out * momentum_out) + jnp.sum(vec_momentum_out * vec_momentum_out)
    scale = 0.05 / jnp.sqrt(total / (2 * D * D + 6 * D) + 1e-06)
    weights_out = weights - scale * momentum_out
    vec_params_out = vec_params - scale * vec_momentum_out
    return (errors_out, p_factor, q_factor, momentum_out, weights_out, vec_momentum_out, vec_params_out)
```

```python
import functools

import jax
import jax.numpy as jnp
from jax import lax
from jax.experimental import pallas as pl
from jax.experimental.pallas import tpu as pltpu
from jax.sharding import PartitionSpec as P

F32 = jnp.float32
BF16 = jnp.bfloat16
MESH = pl.DeviceIdType.MESH
CHUNK_ROWS = 16
CHUNK_COLS = 128


def split(x):
    high = x.astype(BF16)
    return high, (x - high.astype(F32)).astype(BF16)


def mm(a, b, dims=((1,), (0,))):
    return lax.dot_general(a, b, (dims, ((), ())), preferred_element_type=F32)


def left_parts(x):
    high, low = split(x)
    return jnp.concatenate([high, high, low], axis=1)


def right_parts(x):
    high, low = split(x)
    return jnp.concatenate([high, low, high], axis=0)


def each(count, body):
    if count <= 16:
        for i in range(count):
            body(i)
    else:
        lax.fori_loop(0, count, lambda i, c: (body(i), c)[1], 0)


def kernel(
    sizes,
    g_hbm, e_hbm, qt_hbm, pr_hbm, qr_hbm, m_hbm, w_hbm, vg_hbm, vm_hbm, vp_hbm,
    eo_hbm, pt_hbm, qf_hbm, mo_hbm, wo_hbm, vmo_hbm, vpo_hbm,
    g_v, e_v, qt_v, pr_v, qr_v, m_v, w_v, vm_v, vp_v,
    hi_v, lo_v, pbuf, vbuf, qpart, rbuf, qfull, sbuf, pf_v, qf_v,
    in_sem, out_sem, psend, precv, vsend, vrecv, rsend, rrecv, asend, arecv, ssend, srecv,
):
    n_dp, n_t, n_s = sizes
    n = n_dp * n_t
    group = n_t * n_s
    dp, tn, sc = lax.axis_index("dp"), lax.axis_index("tensor"), lax.axis_index("section")
    me = dp * n_t + tn
    rank, width = qt_v.shape
    rows = e_v.shape[0]
    col_chunks = width // CHUNK_COLS
    chunks = (rank // CHUNK_ROWS) * col_chunks
    mine = (me * chunks + n - 1) // n
    owns = jnp.logical_and(mine < chunks, (mine * n) // chunks == me)

    def load(i, src, dst):
        copy = pltpu.make_async_copy(src, dst, in_sem.at[i])
        copy.start()
        return copy

    ins = [
        load(0, g_hbm, g_v),
        load(1, e_hbm, e_v),
        load(2, qt_hbm, qt_v),
        load(3, pr_hbm, pr_v),
        load(4, qr_hbm, qr_v),
        load(5, vg_hbm, vbuf.at[dp]),
        load(6, m_hbm, m_v),
        load(7, vm_hbm, vm_v),
        load(8, w_hbm, w_v),
        load(9, vp_hbm, vp_v),
    ]

    barrier = pltpu.get_barrier_semaphore()

    def greet_group(i):
        peer = lax.rem(me + 1 + i, n)
        pl.semaphore_signal(
            barrier, inc=1, device_id=(peer // n_t, lax.rem(peer, n_t), sc), device_id_type=MESH
        )

    def greet_section(i):
        other = lax.rem(sc + 1 + i // n_t, n_s)
        pl.semaphore_signal(
            barrier, inc=1, device_id=(dp, i % n_t, other), device_id_type=MESH
        )

    each(n - 1, greet_group)
    each((n_s - 1) * n_t, greet_section)

    ins[2].wait()
    q_hi, q_lo = split(qt_v[...])
    ins[0].wait()
    ins[1].wait()
    merged = g_v[...].astype(F32) + e_v[...]
    e_v[...] = merged
    m_hi, m_lo = split(merged)
    hi_v[...] = m_hi
    lo_v[...] = m_lo
    first = mm(jnp.concatenate([q_hi, q_lo], axis=0), hi_v[...], ((1,), (1,)))
    second = mm(q_hi, lo_v[...], ((1,), (1,)))
    pbuf[dp] = first[:rank] + first[rank:] + second

    pl.semaphore_wait(barrier, n - 1 + (n_s - 1) * n_t)
    ins[5].wait()

    def send_p(i):
        peer = lax.rem(dp + 1 + i, n_dp)
        pltpu.make_async_remote_copy(
            pbuf.at[dp], pbuf.at[dp], psend, precv, device_id=(peer, tn, sc), device_id_type=MESH
        ).start()

    def send_v(i):
        peer = lax.rem(dp + 1 + i, n_dp)
        pltpu.make_async_remote_copy(
            vbuf.at[dp], vbuf.at[dp], vsend, vrecv, device_id=(peer, tn, sc), device_id_type=MESH
        ).start()

    each(n_dp - 1, send_p)
    each(n_dp - 1, send_v)

    ins[3].wait()
    ins[4].wait()
    p_root_left = left_parts(pr_v[...].T)
    q_root_left = left_parts(qr_v[...])

    others = pl.ds(0, n_dp - 1)
    pltpu.make_async_copy(pbuf.at[others], pbuf.at[others], precv).wait()
    if n_dp <= 16:
        p_sum = pbuf[0]
        for i in range(1, n_dp):
            p_sum = p_sum + pbuf[i]
    else:
        p_sum = lax.fori_loop(1, n_dp, lambda i, acc: acc + pbuf[i], pbuf[0])
    pf = mm(p_root_left, right_parts(p_sum))
    pf_hi, pf_lo = split(pf)
    pf_both = jnp.concatenate([pf_hi, pf_lo], axis=0)

    def send_chunk(k):
        owner = (k * n) // chunks
        at = (
            pl.ds((k // col_chunks) * CHUNK_ROWS, CHUNK_ROWS),
            pl.ds((k % col_chunks) * CHUNK_COLS, CHUNK_COLS),
        )

        @pl.when(me == owner)
        def _():
            rbuf[me] = qpart[at]

        @pl.when(me != owner)
        def _():
            pltpu.make_async_remote_copy(
                qpart.at[at], rbuf.at[me], rsend, rrecv,
                device_id=(owner // n_t, owner % n_t, sc), device_id_type=MESH,
            ).start()

    block = 2 * CHUNK_COLS
    for c in range(width // block):
        cols = pl.ds(c * block, block)
        first = mm(pf_both, hi_v[:, cols])
        second = mm(pf_hi, lo_v[:, cols])
        qpart[:, cols] = first[:rank] + first[rank:] + second
    for k in range(chunks):
        send_chunk(k)

    pf_v[...] = pf
    p_out = pltpu.make_async_copy(pf_v, pt_hbm, out_sem.at[0])
    p_out.start()
    left = mm(q_root_left, right_parts(pf)).T / n_dp
    left = left_parts(left)

    pltpu.make_async_copy(vbuf.at[others], vbuf.at[others], vrecv).wait()
    if n_dp <= 16:
        v_sum = vbuf[0]
        for i in range(1, n_dp):
            v_sum = v_sum + vbuf[i]
    else:
        v_sum = lax.fori_loop(1, n_dp, lambda i, acc: acc + vbuf[i], vbuf[0])
    ins[7].wait()
    v_new = 0.9 * vm_v[...] + v_sum / n_dp
    vm_v[...] = v_new
    v_out = pltpu.make_async_copy(vm_v, vmo_hbm, out_sem.at[1])
    v_out.start()
    v_square = jnp.sum(v_new * v_new)

    @pl.when(owns)
    def _():
        whole = pl.ds(0, n - 1)
        pltpu.make_async_copy(rbuf.at[whole], rbuf.at[whole], rrecv).wait()
        if n <= 16:
            q_sum = rbuf[0]
            for i in range(1, n):
                q_sum = q_sum + rbuf[i]
        else:
            q_sum = lax.fori_loop(1, n, lambda i, acc: acc + rbuf[i], rbuf[0])
        qfull[mine] = q_sum

        def send_sum(i):
            peer = lax.rem(me + 1 + i, n)
            pltpu.make_async_remote_copy(
                qfull.at[mine], qfull.at[mine], asend, arecv,
                device_id=(peer // n_t, lax.rem(peer, n_t), sc), device_id_type=MESH,
            ).start()

        each(n - 1, send_sum)
        got = pl.ds(0, chunks - 1)
        pltpu.make_async_copy(qfull.at[got], qfull.at[got], arecv).wait()

    @pl.when(jnp.logical_not(owns))
    def _():
        pltpu.make_async_copy(qfull, qfull, arecv).wait()

    ins[6].wait()
    squares = jnp.zeros((8, 128), F32)
    q_parts = []
    for c in range(width // block):
        cols = pl.ds(c * block, block)
        q_sum = jnp.concatenate(
            [
                jnp.concatenate([qfull[r * col_chunks + 2 * c + j] for j in range(2)], axis=1)
                for r in range(rank // CHUNK_ROWS)
            ],
            axis=0,
        )
        right = right_parts(q_sum)
        q_parts.append(right)
        approx = mm(left, right)
        new = 0.9 * m_v[:, cols] + approx
        m_v[:, cols] = new
        e_v[:, cols] = e_v[:, cols] - approx
        square = new * new
        for j in range(2):
            squares = squares + jnp.sum(
                square[:, j * 128 : (j + 1) * 128].reshape(rows // 8, 8, 128), axis=0
            )
    corner = jnp.logical_and(
        lax.broadcasted_iota(jnp.int32, (8, 128), 0) == 0,
        lax.broadcasted_iota(jnp.int32, (8, 128), 1) == 0,
    )
    slot = sc * n_t + tn
    sbuf[slot] = squares + jnp.where(corner, v_square, 0.0)
    for i in range(1, group):
        peer = lax.rem(slot + i, group)
        pltpu.make_async_remote_copy(
            sbuf.at[slot], sbuf.at[slot], ssend, srecv,
            device_id=(dp, lax.rem(peer, n_t), peer // n_t), device_id_type=MESH,
        ).start()
    m_out = pltpu.make_async_copy(m_v, mo_hbm, out_sem.at[2])
    m_out.start()
    e_out = pltpu.make_async_copy(e_v, eo_hbm, out_sem.at[3])
    e_out.start()
    q_root_t = left_parts(qr_v[...].T)
    for c in range(width // block):
        qf_v[:, pl.ds(c * block, block)] = mm(q_root_t, q_parts[c])
    q_out = pltpu.make_async_copy(qf_v, qf_hbm, out_sem.at[4])
    q_out.start()
    ins[8].wait()
    ins[9].wait()

    rest = pl.ds(0, group - 1)
    pltpu.make_async_copy(sbuf.at[rest], sbuf.at[rest], srecv).wait()
    total_tile = sbuf[0]
    for i in range(1, group):
        total_tile = total_tile + sbuf[i]
    total = jnp.sum(jnp.sum(total_tile, axis=1, keepdims=True), axis=0, keepdims=True)
    count = n_s * (width * width + 3 * width)
    scale = 0.05 / jnp.sqrt(total / count + 1e-06)
    outs = [p_out, v_out, m_out, e_out, q_out]
    pieces = 4
    step = rows // pieces
    for i in range(pieces):
        part = pl.ds(i * step, step)
        w_v[part, :] = w_v[part, :] - scale * m_v[part, :]
        copy = pltpu.make_async_copy(w_v.at[part], wo_hbm.at[part], out_sem.at[5 + i])
        copy.start()
        outs.append(copy)
    vp_v[...] = vp_v[...] - scale.reshape(1, 1, 1) * vm_v[...]
    copy = pltpu.make_async_copy(vp_v, vpo_hbm, out_sem.at[5 + pieces])
    copy.start()
    outs.append(copy)

    pltpu.make_async_copy(pbuf.at[others], pbuf.at[others], psend).wait()
    pltpu.make_async_copy(vbuf.at[others], vbuf.at[others], vsend).wait()
    pltpu.make_async_copy(sbuf.at[rest], sbuf.at[rest], ssend).wait()

    @pl.when(owns)
    def _():
        got = pl.ds(0, chunks - 1)
        pltpu.make_async_copy(qfull.at[got], qfull.at[got], rsend).wait()
        whole = pl.ds(0, n - 1)
        pltpu.make_async_copy(rbuf.at[whole], rbuf.at[whole], asend).wait()

    @pl.when(jnp.logical_not(owns))
    def _():
        pltpu.make_async_copy(qfull, qfull, rsend).wait()

    for copy in outs:
        copy.wait()


def shards(
    sizes,
    grads, errors, q_prev, p_root, q_root, momentum, weights, vec_grads, vec_momentum, vec_params,
):
    n_dp, n_t, n_s = sizes
    rows, width = errors.shape[2:]
    rank = q_prev.shape[2]
    vecs, entries = vec_params.shape[1:]
    n = n_dp * n_t
    chunks = (rank // CHUNK_ROWS) * (width // CHUNK_COLS)
    big = jax.ShapeDtypeStruct((rows, width), F32)
    vec = jax.ShapeDtypeStruct((vecs, 1, entries), F32)
    any_space = pl.BlockSpec(memory_space=pl.ANY)
    dma = pltpu.SemaphoreType.DMA
    vmem = pltpu.VMEM
    outs = pl.pallas_call(
        functools.partial(kernel, sizes),
        out_shape=(
            big,
            jax.ShapeDtypeStruct((rank, rows), F32),
            jax.ShapeDtypeStruct((rank, width), F32),
            big,
            big,
            vec,
            vec,
        ),
        in_specs=[pl.BlockSpec(memory_space=pltpu.HBM)] * 10,
        out_specs=(any_space,) * 7,
        scratch_shapes=[
            vmem((rows, width), BF16),
            vmem((rows, width), F32),
            vmem((rank, width), F32),
            vmem((rank, rank), F32),
            vmem((rank, rank), F32),
            vmem((rows, width), F32),
            vmem((rows, width), F32),
            vmem((vecs, 1, entries), F32),
            vmem((vecs, 1, entries), F32),
            vmem((rows, width), BF16),
            vmem((rows, width), BF16),
            vmem((n_dp, rank, rows), F32),
            vmem((n_dp, vecs, 1, entries), F32),
            vmem((rank, width), F32),
            vmem((n, CHUNK_ROWS, CHUNK_COLS), F32),
            vmem((chunks, CHUNK_ROWS, CHUNK_COLS), F32),
            vmem((n_t * n_s, 8, 128), F32),
            vmem((rank, rows), F32),
            vmem((rank, width), F32),
            dma((10,)),
            dma((10,)),
        ]
        + [dma(())] * 10,
        compiler_params=pltpu.CompilerParams(
            collective_id=0, has_side_effects=True, vmem_limit_bytes=48 * 1024 * 1024
        ),
    )(
        grads[0, 0],
        errors[0, 0],
        q_prev[0].T,
        p_root[0],
        q_root[0],
        momentum[0],
        weights[0],
        vec_grads[0, 0][:, None, :],
        vec_momentum[0][:, None, :],
        vec_params[0][:, None, :],
    )
    errors_out, p_factor, q_factor, momentum_out, weights_out, vec_momentum_out, vec_params_out = outs
    return (
        errors_out[None, None],
        p_factor.T[None],
        q_factor.T[None],
        momentum_out[None],
        weights_out[None],
        vec_momentum_out[:, 0][None],
        vec_params_out[:, 0][None],
    )


def solution(mesh):
    sizes = (mesh.shape["dp"], mesh.shape["tensor"], mesh.shape["section"])
    in_specs = (
        P("dp", "section", "tensor", None),
        P("dp", "section", "tensor", None),
        P("section", None, None),
        P("section", None, None),
        P("section", None, None),
        P("section", "tensor", None),
        P("section", "tensor", None),
        P("dp", "section", None, "tensor"),
        P("section", None, "tensor"),
        P("section", None, "tensor"),
    )
    out_specs = (
        P("dp", "section", "tensor", None),
        P("section", "tensor", None),
        P("section", None, None),
        P("section", "tensor", None),
        P("section", "tensor", None),
        P("section", None, "tensor"),
        P("section", None, "tensor"),
    )
    return jax.shard_map(
        functools.partial(shards, sizes),
        mesh=mesh, in_specs=in_specs, out_specs=out_specs, check_vma=False,
    )
```

```python
import functools

import jax
import jax.numpy as jnp
from jax import lax
from jax.experimental import pallas as pl
from jax.experimental.pallas import tpu as pltpu
from jax.sharding import PartitionSpec as P

F32 = jnp.float32
BF16 = jnp.bfloat16
MESH = pl.DeviceIdType.MESH
CHUNK_ROWS = 16
CHUNK_COLS = 128


def split(x):
    high = x.astype(BF16)
    return high, (x - high.astype(F32)).astype(BF16)


def mm(a, b, dims=((1,), (0,))):
    return lax.dot_general(a, b, (dims, ((), ())), preferred_element_type=F32)


def left_parts(x):
    high, low = split(x)
    return jnp.concatenate([high, high, low], axis=1)


def right_parts(x):
    high, low = split(x)
    return jnp.concatenate([high, low, high], axis=0)


def each(count, body):
    if count <= 16:
        for i in range(count):
            body(i)
    else:
        lax.fori_loop(0, count, lambda i, c: (body(i), c)[1], 0)


def kernel(
    sizes,
    g_hbm, e_hbm, qt_hbm, pr_hbm, qr_hbm, m_hbm, w_hbm, vg_hbm, vm_hbm, vp_hbm,
    eo_v, pf_v, qf_v, mo_v, wo_v, vmo_v, vpo_v,
    g_v, e_v, qt_v, pr_v, qr_v, m_v, w_v, vm_v, vp_v,
    hi_v, lo_v, pbuf, vbuf, qpart, rbuf, qfull, sbuf,
    in_sem, psend, precv, vsend, vrecv, rsend, rrecv, asend, arecv, ssend, srecv,
):
    n_dp, n_t, n_s = sizes
    n = n_dp * n_t
    group = n_t * n_s
    dp, tn, sc = lax.axis_index("dp"), lax.axis_index("tensor"), lax.axis_index("section")
    me = dp * n_t + tn
    rank, width = qt_v.shape
    rows = e_v.shape[0]
    col_chunks = width // CHUNK_COLS
    chunks = (rank // CHUNK_ROWS) * col_chunks
    mine = (me * chunks + n - 1) // n
    owns = jnp.logical_and(mine < chunks, (mine * n) // chunks == me)

    def load(i, src, dst):
        copy = pltpu.make_async_copy(src, dst, in_sem.at[i])
        copy.start()
        return copy

    ins = [
        load(0, g_hbm, g_v),
        load(1, e_hbm, e_v),
        load(2, qt_hbm, qt_v),
        load(3, pr_hbm, pr_v),
        load(4, qr_hbm, qr_v),
        load(5, vg_hbm, vbuf.at[dp]),
        load(6, m_hbm, m_v),
        load(7, vm_hbm, vm_v),
        load(8, w_hbm, w_v),
        load(9, vp_hbm, vp_v),
    ]

    barrier = pltpu.get_barrier_semaphore()

    def greet_group(i):
        peer = lax.rem(me + 1 + i, n)
        pl.semaphore_signal(
            barrier, inc=1, device_id=(peer // n_t, lax.rem(peer, n_t), sc), device_id_type=MESH
        )

    def greet_section(i):
        other = lax.rem(sc + 1 + i // n_t, n_s)
        pl.semaphore_signal(
            barrier, inc=1, device_id=(dp, i % n_t, other), device_id_type=MESH
        )

    each(n - 1, greet_group)
    each((n_s - 1) * n_t, greet_section)

    ins[2].wait()
    q_hi, q_lo = split(qt_v[...])
    ins[0].wait()
    ins[1].wait()
    merged = g_v[...].astype(F32) + e_v[...]
    e_v[...] = merged
    m_hi, m_lo = split(merged)
    hi_v[...] = m_hi
    lo_v[...] = m_lo
    first = mm(jnp.concatenate([q_hi, q_lo], axis=0), hi_v[...], ((1,), (1,)))
    second = mm(q_hi, lo_v[...], ((1,), (1,)))
    pbuf[dp] = first[:rank] + first[rank:] + second

    pl.semaphore_wait(barrier, n - 1 + (n_s - 1) * n_t)
    ins[5].wait()

    def send_p(i):
        peer = lax.rem(dp + 1 + i, n_dp)
        pltpu.make_async_remote_copy(
            pbuf.at[dp], pbuf.at[dp], psend, precv, device_id=(peer, tn, sc), device_id_type=MESH
        ).start()

    def send_v(i):
        peer = lax.rem(dp + 1 + i, n_dp)
        pltpu.make_async_remote_copy(
            vbuf.at[dp], vbuf.at[dp], vsend, vrecv, device_id=(peer, tn, sc), device_id_type=MESH
        ).start()

    each(n_dp - 1, send_p)
    each(n_dp - 1, send_v)

    ins[3].wait()
    ins[4].wait()
    p_root_left = left_parts(pr_v[...].T)
    q_root_left = left_parts(qr_v[...])

    others = pl.ds(0, n_dp - 1)
    pltpu.make_async_copy(pbuf.at[others], pbuf.at[others], precv).wait()
    if n_dp <= 16:
        p_sum = pbuf[0]
        for i in range(1, n_dp):
            p_sum = p_sum + pbuf[i]
    else:
        p_sum = lax.fori_loop(1, n_dp, lambda i, acc: acc + pbuf[i], pbuf[0])
    pf = mm(p_root_left, right_parts(p_sum))
    pf_hi, pf_lo = split(pf)
    pf_both = jnp.concatenate([pf_hi, pf_lo], axis=0)

    def send_chunk(k):
        owner = (k * n) // chunks
        at = (
            pl.ds((k // col_chunks) * CHUNK_ROWS, CHUNK_ROWS),
            pl.ds((k % col_chunks) * CHUNK_COLS, CHUNK_COLS),
        )

        @pl.when(me == owner)
        def _():
            rbuf[me] = qpart[at]

        @pl.when(me != owner)
        def _():
            pltpu.make_async_remote_copy(
                qpart.at[at], rbuf.at[me], rsend, rrecv,
                device_id=(owner // n_t, owner % n_t, sc), device_id_type=MESH,
            ).start()

    block = 2 * CHUNK_COLS
    for c in range(width // block):
        cols = pl.ds(c * block, block)
        first = mm(pf_both, hi_v[:, cols])
        second = mm(pf_hi, lo_v[:, cols])
        qpart[:, cols] = first[:rank] + first[rank:] + second
    for k in range(chunks):
        send_chunk(k)

    pf_v[...] = pf
    left = mm(q_root_left, right_parts(pf)).T / n_dp
    left = left_parts(left)

    pltpu.make_async_copy(vbuf.at[others], vbuf.at[others], vrecv).wait()
    if n_dp <= 16:
        v_sum = vbuf[0]
        for i in range(1, n_dp):
            v_sum = v_sum + vbuf[i]
    else:
        v_sum = lax.fori_loop(1, n_dp, lambda i, acc: acc + vbuf[i], vbuf[0])
    ins[7].wait()
    v_new = 0.9 * vm_v[...] + v_sum / n_dp
    vmo_v[...] = v_new
    v_square = jnp.sum(v_new * v_new)

    @pl.when(owns)
    def _():
        whole = pl.ds(0, n - 1)
        pltpu.make_async_copy(rbuf.at[whole], rbuf.at[whole], rrecv).wait()
        if n <= 16:
            q_sum = rbuf[0]
            for i in range(1, n):
                q_sum = q_sum + rbuf[i]
        else:
            q_sum = lax.fori_loop(1, n, lambda i, acc: acc + rbuf[i], rbuf[0])
        qfull[mine] = q_sum

        def send_sum(i):
            peer = lax.rem(me + 1 + i, n)
            pltpu.make_async_remote_copy(
                qfull.at[mine], qfull.at[mine], asend, arecv,
                device_id=(peer // n_t, lax.rem(peer, n_t), sc), device_id_type=MESH,
            ).start()

        each(n - 1, send_sum)
        got = pl.ds(0, chunks - 1)
        pltpu.make_async_copy(qfull.at[got], qfull.at[got], arecv).wait()

    @pl.when(jnp.logical_not(owns))
    def _():
        pltpu.make_async_copy(qfull, qfull, arecv).wait()

    ins[6].wait()
    squares = jnp.zeros((8, 128), F32)
    q_parts = []
    for c in range(width // block):
        cols = pl.ds(c * block, block)
        q_sum = jnp.concatenate(
            [
                jnp.concatenate([qfull[r * col_chunks + 2 * c + j] for j in range(2)], axis=1)
                for r in range(rank // CHUNK_ROWS)
            ],
            axis=0,
        )
        right = right_parts(q_sum)
        q_parts.append(right)
        approx = mm(left, right)
        new = 0.9 * m_v[:, cols] + approx
        mo_v[:, cols] = new
        square = new * new
        for j in range(2):
            squares = squares + jnp.sum(
                square[:, j * 128 : (j + 1) * 128].reshape(rows // 8, 8, 128), axis=0
            )
    corner = jnp.logical_and(
        lax.broadcasted_iota(jnp.int32, (8, 128), 0) == 0,
        lax.broadcasted_iota(jnp.int32, (8, 128), 1) == 0,
    )
    slot = sc * n_t + tn
    sbuf[slot] = squares + jnp.where(corner, v_square, 0.0)
    for i in range(1, group):
        peer = lax.rem(slot + i, group)
        pltpu.make_async_remote_copy(
            sbuf.at[slot], sbuf.at[slot], ssend, srecv,
            device_id=(dp, lax.rem(peer, n_t), peer // n_t), device_id_type=MESH,
        ).start()
    q_root_t = left_parts(qr_v[...].T)
    for c in range(width // block):
        cols = pl.ds(c * block, block)
        eo_v[:, cols] = e_v[:, cols] - mm(left, q_parts[c])
        qf_v[:, cols] = mm(q_root_t, q_parts[c])
    ins[8].wait()
    ins[9].wait()

    rest = pl.ds(0, group - 1)
    pltpu.make_async_copy(sbuf.at[rest], sbuf.at[rest], srecv).wait()
    total_tile = sbuf[0]
    for i in range(1, group):
        total_tile = total_tile + sbuf[i]
    total = jnp.sum(jnp.sum(total_tile, axis=1, keepdims=True), axis=0, keepdims=True)
    count = n_s * (width * width + 3 * width)
    scale = 0.05 / jnp.sqrt(total / count + 1e-06)
    wo_v[...] = w_v[...] - scale * mo_v[...]
    vpo_v[...] = vp_v[...] - scale.reshape(1, 1, 1) * vmo_v[...]

    pltpu.make_async_copy(pbuf.at[others], pbuf.at[others], psend).wait()
    pltpu.make_async_copy(vbuf.at[others], vbuf.at[others], vsend).wait()
    pltpu.make_async_copy(sbuf.at[rest], sbuf.at[rest], ssend).wait()

    @pl.when(owns)
    def _():
        got = pl.ds(0, chunks - 1)
        pltpu.make_async_copy(qfull.at[got], qfull.at[got], rsend).wait()
        whole = pl.ds(0, n - 1)
        pltpu.make_async_copy(rbuf.at[whole], rbuf.at[whole], asend).wait()

    @pl.when(jnp.logical_not(owns))
    def _():
        pltpu.make_async_copy(qfull, qfull, rsend).wait()


def write(count, *refs):
    sems = refs[2 * count]
    copies = [
        pltpu.make_async_copy(refs[i], refs[count + i], sems.at[i]) for i in range(count)
    ]
    for copy in copies:
        copy.start()
    for copy in copies:
        copy.wait()


def shards(
    sizes,
    grads, errors, q_prev, p_root, q_root, momentum, weights, vec_grads, vec_momentum, vec_params,
):
    n_dp, n_t, n_s = sizes
    rows, width = errors.shape[2:]
    rank = q_prev.shape[2]
    vecs, entries = vec_params.shape[1:]
    n = n_dp * n_t
    chunks = (rank // CHUNK_ROWS) * (width // CHUNK_COLS)
    big = (rows, width)
    vec = (vecs, 1, entries)
    shapes = (big, (rank, rows), (rank, width), big, big, vec, vec)
    any_space = pl.BlockSpec(memory_space=pl.ANY)
    in_vmem = pl.BlockSpec(memory_space=pltpu.VMEM)
    dma = pltpu.SemaphoreType.DMA
    vmem = pltpu.VMEM
    args = (
        grads[0, 0],
        errors[0, 0],
        q_prev[0].T,
        p_root[0],
        q_root[0],
        momentum[0],
        weights[0],
        vec_grads[0, 0][:, None, :],
        vec_momentum[0][:, None, :],
        vec_params[0][:, None, :],
    )
    outs = pl.pallas_call(
        functools.partial(kernel, sizes),
        out_shape=tuple(vmem(shape, F32) for shape in shapes),
        in_specs=[any_space] * 10,
        out_specs=(in_vmem,) * 7,
        scratch_shapes=[
            vmem((rows, width), BF16),
            vmem((rows, width), F32),
            vmem((rank, width), F32),
            vmem((rank, rank), F32),
            vmem((rank, rank), F32),
            vmem((rows, width), F32),
            vmem((rows, width), F32),
            vmem((vecs, 1, entries), F32),
            vmem((vecs, 1, entries), F32),
            vmem((rows, width), BF16),
            vmem((rows, width), BF16),
            vmem((n_dp, rank, rows), F32),
            vmem((n_dp, vecs, 1, entries), F32),
            vmem((rank, width), F32),
            vmem((n, CHUNK_ROWS, CHUNK_COLS), F32),
            vmem((chunks, CHUNK_ROWS, CHUNK_COLS), F32),
            vmem((n_t * n_s, 8, 128), F32),
            dma((10,)),
        ]
        + [dma(())] * 10,
        compiler_params=pltpu.CompilerParams(
            collective_id=0, has_side_effects=True, vmem_limit_bytes=48 * 1024 * 1024
        ),
    )(*(pltpu.with_memory_space_constraint(arg, pltpu.HBM) for arg in args))
    outs = pl.pallas_call(
        functools.partial(write, 7),
        out_shape=tuple(pltpu.HBM(shape, F32) for shape in shapes),
        in_specs=[in_vmem] * 7,
        out_specs=(any_space,) * 7,
        scratch_shapes=[dma((7,))],
    )(*(pltpu.with_memory_space_constraint(out, pltpu.VMEM) for out in outs))
    errors_out, p_factor, q_factor, momentum_out, weights_out, vec_momentum_out, vec_params_out = outs
    return (
        errors_out[None, None],
        p_factor.T[None],
        q_factor.T[None],
        momentum_out[None],
        weights_out[None],
        vec_momentum_out[:, 0][None],
        vec_params_out[:, 0][None],
    )


def solution(mesh):
    sizes = (mesh.shape["dp"], mesh.shape["tensor"], mesh.shape["section"])
    in_specs = (
        P("dp", "section", "tensor", None),
        P("dp", "section", "tensor", None),
        P("section", None, None),
        P("section", None, None),
        P("section", None, None),
        P("section", "tensor", None),
        P("section", "tensor", None),
        P("dp", "section", None, "tensor"),
        P("section", None, "tensor"),
        P("section", None, "tensor"),
    )
    out_specs = (
        P("dp", "section", "tensor", None),
        P("section", "tensor", None),
        P("section", None, None),
        P("section", "tensor", None),
        P("section", "tensor", None),
        P("section", None, "tensor"),
        P("section", None, "tensor"),
    )
    return jax.shard_map(
        functools.partial(shards, sizes),
        mesh=mesh, in_specs=in_specs, out_specs=out_specs, check_vma=False,
    )
```

```python
import functools

import jax
import jax.numpy as jnp
from jax import lax
from jax.experimental import pallas as pl
from jax.experimental.pallas import tpu as pltpu
from jax.sharding import PartitionSpec as P

F32 = jnp.float32
BF16 = jnp.bfloat16
MESH = pl.DeviceIdType.MESH
CHUNK_ROWS = 16
CHUNK_COLS = 128


def split(x):
    high = x.astype(BF16)
    return high, (x - high.astype(F32)).astype(BF16)


def mm(a, b, dims=((1,), (0,))):
    return lax.dot_general(a, b, (dims, ((), ())), preferred_element_type=F32)


def left_parts(x):
    high, low = split(x)
    return jnp.concatenate([high, high, low], axis=1)


def right_parts(x):
    high, low = split(x)
    return jnp.concatenate([high, low, high], axis=0)


def each(count, body):
    if count <= 16:
        for i in range(count):
            body(i)
    else:
        lax.fori_loop(0, count, lambda i, c: (body(i), c)[1], 0)


def kernel(
    sizes,
    g_hbm, e_hbm, qt_hbm, pr_hbm, qr_hbm, m_hbm, w_hbm, vg_hbm, vm_hbm, vp_hbm,
    eo_v, pf_v, qf_v, mo_v, wo_v, vmo_v, vpo_v,
    g_v, e_v, qt_v, pr_v, qr_v, m_v, w_v, vm_v, vp_v,
    hi_v, lo_v, pbuf, vbuf, qpart, rbuf, qfull, sbuf,
    in_sem, psend, precv, vsend, vrecv, rsend, rrecv, asend, arecv, ssend, srecv,
):
    n_dp, n_t, n_s = sizes
    n = n_dp * n_t
    group = n_t * n_s
    dp, tn, sc = lax.axis_index("dp"), lax.axis_index("tensor"), lax.axis_index("section")
    me = dp * n_t + tn
    rank, width = qt_v.shape
    rows = e_v.shape[0]
    col_chunks = width // CHUNK_COLS
    chunks = (rank // CHUNK_ROWS) * col_chunks
    mine = (me * chunks + n - 1) // n
    owns = jnp.logical_and(mine < chunks, (mine * n) // chunks == me)

    def load(i, src, dst):
        copy = pltpu.make_async_copy(src, dst, in_sem.at[i])
        copy.start()
        return copy

    ins = [
        load(0, g_hbm, g_v),
        load(1, e_hbm, e_v),
        load(2, qt_hbm, qt_v),
        load(3, pr_hbm, pr_v),
        load(4, qr_hbm, qr_v),
        load(5, vg_hbm, vbuf.at[dp]),
        load(6, m_hbm, m_v),
        load(7, vm_hbm, vm_v),
        load(8, w_hbm, w_v),
        load(9, vp_hbm, vp_v),
    ]

    barrier = pltpu.get_barrier_semaphore()
    slot = sc * n_t + tn

    def greet_line(i):
        pl.semaphore_signal(
            barrier, inc=1, device_id=(lax.rem(dp + 1 + i, n_dp), tn, sc), device_id_type=MESH
        )

    def greet_plane(i):
        peer = lax.rem(slot + 1 + i, group)
        pl.semaphore_signal(
            barrier, inc=1, device_id=(dp, lax.rem(peer, n_t), peer // n_t), device_id_type=MESH
        )

    each(n_dp - 1, greet_line)
    each(group - 1, greet_plane)

    ins[2].wait()
    q_hi, q_lo = split(qt_v[...])
    ins[0].wait()
    ins[1].wait()
    merged = g_v[...].astype(F32) + e_v[...]
    e_v[...] = merged
    m_hi, m_lo = split(merged)
    hi_v[...] = m_hi
    lo_v[...] = m_lo
    first = mm(jnp.concatenate([q_hi, q_lo], axis=0), hi_v[...], ((1,), (1,)))
    second = mm(q_hi, lo_v[...], ((1,), (1,)))
    pbuf[dp] = first[:rank] + first[rank:] + second

    pl.semaphore_wait(barrier, n_dp - 1 + group - 1)
    ins[5].wait()

    def send_p(i):
        peer = lax.rem(dp + 1 + i, n_dp)
        pltpu.make_async_remote_copy(
            pbuf.at[dp], pbuf.at[dp], psend, precv, device_id=(peer, tn, sc), device_id_type=MESH
        ).start()

    def send_v(i):
        peer = lax.rem(dp + 1 + i, n_dp)
        pltpu.make_async_remote_copy(
            vbuf.at[dp], vbuf.at[dp], vsend, vrecv, device_id=(peer, tn, sc), device_id_type=MESH
        ).start()

    each(n_dp - 1, send_p)

    ins[3].wait()
    ins[4].wait()
    p_root_left = left_parts(pr_v[...].T)
    q_root_left = left_parts(qr_v[...])

    others = pl.ds(0, n_dp - 1)
    pltpu.make_async_copy(pbuf.at[others], pbuf.at[others], precv).wait()
    if n_dp <= 16:
        p_sum = pbuf[0]
        for i in range(1, n_dp):
            p_sum = p_sum + pbuf[i]
    else:
        p_sum = lax.fori_loop(1, n_dp, lambda i, acc: acc + pbuf[i], pbuf[0])
    pf = mm(p_root_left, right_parts(p_sum))
    pf_hi, pf_lo = split(pf)
    pf_both = jnp.concatenate([pf_hi, pf_lo], axis=0)

    def send_chunk(k):
        owner = (k * n) // chunks
        at = (
            pl.ds((k // col_chunks) * CHUNK_ROWS, CHUNK_ROWS),
            pl.ds((k % col_chunks) * CHUNK_COLS, CHUNK_COLS),
        )

        @pl.when(me == owner)
        def _():
            rbuf[me] = qpart[at]

        @pl.when(me != owner)
        def _():
            pltpu.make_async_remote_copy(
                qpart.at[at], rbuf.at[me], rsend, rrecv,
                device_id=(owner // n_t, owner % n_t, sc), device_id_type=MESH,
            ).start()

    block = 2 * CHUNK_COLS
    for c in range(width // block):
        cols = pl.ds(c * block, block)
        first = mm(pf_both, hi_v[:, cols])
        second = mm(pf_hi, lo_v[:, cols])
        qpart[:, cols] = first[:rank] + first[rank:] + second
        for r in range(rank // CHUNK_ROWS):
            for j in range(2):
                send_chunk(r * col_chunks + 2 * c + j)
    each(n_dp - 1, send_v)

    pf_v[...] = pf
    left = mm(q_root_left, right_parts(pf)).T / n_dp
    left = left_parts(left)

    @pl.when(owns)
    def _():
        whole = pl.ds(0, n - 1)
        pltpu.make_async_copy(rbuf.at[whole], rbuf.at[whole], rrecv).wait()
        if n <= 16:
            q_sum = rbuf[0]
            for i in range(1, n):
                q_sum = q_sum + rbuf[i]
        else:
            q_sum = lax.fori_loop(1, n, lambda i, acc: acc + rbuf[i], rbuf[0])
        qfull[mine] = q_sum

        def send_sum(i):
            peer = lax.rem(2 * n - 1 - me + i, n)

            @pl.when(peer != me)
            def _():
                send_sum_to(peer)

        def send_sum_to(peer):
            pltpu.make_async_remote_copy(
                qfull.at[mine], qfull.at[mine], asend, arecv,
                device_id=(peer // n_t, lax.rem(peer, n_t), sc), device_id_type=MESH,
            ).start()

        each(n, send_sum)
        got = pl.ds(0, chunks - 1)
        pltpu.make_async_copy(qfull.at[got], qfull.at[got], arecv).wait()

    @pl.when(jnp.logical_not(owns))
    def _():
        pltpu.make_async_copy(qfull, qfull, arecv).wait()

    ins[6].wait()
    squares = jnp.zeros((8, 128), F32)
    q_parts = []
    for c in range(width // block):
        cols = pl.ds(c * block, block)
        q_sum = jnp.concatenate(
            [
                jnp.concatenate([qfull[r * col_chunks + 2 * c + j] for j in range(2)], axis=1)
                for r in range(rank // CHUNK_ROWS)
            ],
            axis=0,
        )
        right = right_parts(q_sum)
        q_parts.append(right)
        approx = mm(left, right)
        new = 0.9 * m_v[:, cols] + approx
        mo_v[:, cols] = new
        square = new * new
        for j in range(2):
            squares = squares + jnp.sum(
                square[:, j * 128 : (j + 1) * 128].reshape(rows // 8, 8, 128), axis=0
            )
    pltpu.make_async_copy(vbuf.at[others], vbuf.at[others], vrecv).wait()
    if n_dp <= 16:
        v_sum = vbuf[0]
        for i in range(1, n_dp):
            v_sum = v_sum + vbuf[i]
    else:
        v_sum = lax.fori_loop(1, n_dp, lambda i, acc: acc + vbuf[i], vbuf[0])
    ins[7].wait()
    v_new = 0.9 * vm_v[...] + v_sum / n_dp
    vmo_v[...] = v_new
    v_square = jnp.sum(v_new * v_new)

    corner = jnp.logical_and(
        lax.broadcasted_iota(jnp.int32, (8, 128), 0) == 0,
        lax.broadcasted_iota(jnp.int32, (8, 128), 1) == 0,
    )
    sbuf[slot] = squares + jnp.where(corner, v_square, 0.0)
    for i in range(1, group):
        peer = lax.rem(slot + i, group)
        pltpu.make_async_remote_copy(
            sbuf.at[slot], sbuf.at[slot], ssend, srecv,
            device_id=(dp, lax.rem(peer, n_t), peer // n_t), device_id_type=MESH,
        ).start()
    q_root_t = left_parts(qr_v[...].T)
    for c in range(width // block):
        cols = pl.ds(c * block, block)
        eo_v[:, cols] = e_v[:, cols] - mm(left, q_parts[c])
        qf_v[:, cols] = mm(q_root_t, q_parts[c])
    ins[8].wait()
    ins[9].wait()

    rest = pl.ds(0, group - 1)
    pltpu.make_async_copy(sbuf.at[rest], sbuf.at[rest], srecv).wait()
    total_tile = sbuf[0]
    for i in range(1, group):
        total_tile = total_tile + sbuf[i]
    total = jnp.sum(jnp.sum(total_tile, axis=1, keepdims=True), axis=0, keepdims=True)
    count = n_s * (width * width + 3 * width)
    scale = 0.05 / jnp.sqrt(total / count + 1e-06)
    wo_v[...] = w_v[...] - scale * mo_v[...]
    vpo_v[...] = vp_v[...] - scale.reshape(1, 1, 1) * vmo_v[...]

    pltpu.make_async_copy(pbuf.at[others], pbuf.at[others], psend).wait()
    pltpu.make_async_copy(vbuf.at[others], vbuf.at[others], vsend).wait()
    pltpu.make_async_copy(sbuf.at[rest], sbuf.at[rest], ssend).wait()

    @pl.when(owns)
    def _():
        got = pl.ds(0, chunks - 1)
        pltpu.make_async_copy(qfull.at[got], qfull.at[got], rsend).wait()
        whole = pl.ds(0, n - 1)
        pltpu.make_async_copy(rbuf.at[whole], rbuf.at[whole], asend).wait()

    @pl.when(jnp.logical_not(owns))
    def _():
        pltpu.make_async_copy(qfull, qfull, rsend).wait()


def write(count, *refs):
    sems = refs[2 * count]
    copies = [
        pltpu.make_async_copy(refs[i], refs[count + i], sems.at[i]) for i in range(count)
    ]
    for copy in copies:
        copy.start()
    for copy in copies:
        copy.wait()


def shards(
    sizes,
    grads, errors, q_prev, p_root, q_root, momentum, weights, vec_grads, vec_momentum, vec_params,
):
    n_dp, n_t, n_s = sizes
    rows, width = errors.shape[2:]
    rank = q_prev.shape[2]
    vecs, entries = vec_params.shape[1:]
    n = n_dp * n_t
    chunks = (rank // CHUNK_ROWS) * (width // CHUNK_COLS)
    big = (rows, width)
    vec = (vecs, 1, entries)
    shapes = (big, (rank, rows), (rank, width), big, big, vec, vec)
    any_space = pl.BlockSpec(memory_space=pl.ANY)
    in_vmem = pl.BlockSpec(memory_space=pltpu.VMEM)
    dma = pltpu.SemaphoreType.DMA
    vmem = pltpu.VMEM
    args = (
        grads[0, 0],
        errors[0, 0],
        q_prev[0].T,
        p_root[0],
        q_root[0],
        momentum[0],
        weights[0],
        vec_grads[0, 0][:, None, :],
        vec_momentum[0][:, None, :],
        vec_params[0][:, None, :],
    )
    outs = pl.pallas_call(
        functools.partial(kernel, sizes),
        out_shape=tuple(vmem(shape, F32) for shape in shapes),
        in_specs=[any_space] * 10,
        out_specs=(in_vmem,) * 7,
        scratch_shapes=[
            vmem((rows, width), BF16),
            vmem((rows, width), F32),
            vmem((rank, width), F32),
            vmem((rank, rank), F32),
            vmem((rank, rank), F32),
            vmem((rows, width), F32),
            vmem((rows, width), F32),
            vmem((vecs, 1, entries), F32),
            vmem((vecs, 1, entries), F32),
            vmem((rows, width), BF16),
            vmem((rows, width), BF16),
            vmem((n_dp, rank, rows), F32),
            vmem((n_dp, vecs, 1, entries), F32),
            vmem((rank, width), F32),
            vmem((n, CHUNK_ROWS, CHUNK_COLS), F32),
            vmem((chunks, CHUNK_ROWS, CHUNK_COLS), F32),
            vmem((n_t * n_s, 8, 128), F32),
            dma((10,)),
        ]
        + [dma(())] * 10,
        compiler_params=pltpu.CompilerParams(
            collective_id=0, has_side_effects=True, vmem_limit_bytes=48 * 1024 * 1024
        ),
    )(*(pltpu.with_memory_space_constraint(arg, pltpu.HBM) for arg in args))
    outs = pl.pallas_call(
        functools.partial(write, 7),
        out_shape=tuple(pltpu.HBM(shape, F32) for shape in shapes),
        in_specs=[in_vmem] * 7,
        out_specs=(any_space,) * 7,
        scratch_shapes=[dma((7,))],
    )(*(pltpu.with_memory_space_constraint(out, pltpu.VMEM) for out in outs))
    errors_out, p_factor, q_factor, momentum_out, weights_out, vec_momentum_out, vec_params_out = outs
    return (
        errors_out[None, None],
        p_factor.T[None],
        q_factor.T[None],
        momentum_out[None],
        weights_out[None],
        vec_momentum_out[:, 0][None],
        vec_params_out[:, 0][None],
    )


def solution(mesh):
    sizes = (mesh.shape["dp"], mesh.shape["tensor"], mesh.shape["section"])
    in_specs = (
        P("dp", "section", "tensor", None),
        P("dp", "section", "tensor", None),
        P("section", None, None),
        P("section", None, None),
        P("section", None, None),
        P("section", "tensor", None),
        P("section", "tensor", None),
        P("dp", "section", None, "tensor"),
        P("section", None, "tensor"),
        P("section", None, "tensor"),
    )
    out_specs = (
        P("dp", "section", "tensor", None),
        P("section", "tensor", None),
        P("section", None, None),
        P("section", "tensor", None),
        P("section", "tensor", None),
        P("section", None, "tensor"),
        P("section", None, "tensor"),
    )
    return jax.shard_map(
        functools.partial(shards, sizes),
        mesh=mesh, in_specs=in_specs, out_specs=out_specs, check_vma=False,
    )
```

```python
import functools

import jax
import jax.numpy as jnp
from jax import lax
from jax.experimental import pallas as pl
from jax.experimental.pallas import tpu as pltpu
from jax.sharding import PartitionSpec as P

F32 = jnp.float32
BF16 = jnp.bfloat16
MESH = pl.DeviceIdType.MESH
CHUNK_ROWS = 32
CHUNK_COLS = 128


def split(x):
    high = x.astype(BF16)
    return high, (x - high.astype(F32)).astype(BF16)


def mm(a, b, dims=((1,), (0,))):
    return lax.dot_general(a, b, (dims, ((), ())), preferred_element_type=F32)


def left_parts(x):
    high, low = split(x)
    return jnp.concatenate([high, high, low], axis=1)


def right_parts(x):
    high, low = split(x)
    return jnp.concatenate([high, low, high], axis=0)


def each(count, body):
    if count <= 16:
        for i in range(count):
            body(i)
    else:
        lax.fori_loop(0, count, lambda i, c: (body(i), c)[1], 0)


def kernel(
    sizes,
    g_hbm, e_hbm, qt_hbm, pr_hbm, qr_hbm, m_hbm, w_hbm, vg_hbm, vm_hbm, vp_hbm,
    eo_v, pf_v, qf_v, mo_v, wo_v, vmo_v, vpo_v,
    g_v, e_v, qt_v, pr_v, qr_v, m_v, w_v, vm_v, vp_v,
    hi_v, lo_v, pbuf, vbuf, qpart, rbuf, qfull, sbuf,
    in_sem, psend, precv, vsend, vrecv, rsend, rrecv, asend, arecv, ssend, srecv,
):
    n_dp, n_t, n_s = sizes
    n = n_dp * n_t
    group = n_t * n_s
    dp, tn, sc = lax.axis_index("dp"), lax.axis_index("tensor"), lax.axis_index("section")
    me = dp * n_t + tn
    rank, width = qt_v.shape
    rows = e_v.shape[0]
    col_chunks = width // CHUNK_COLS
    chunks = (rank // CHUNK_ROWS) * col_chunks
    mine = (me * chunks + n - 1) // n
    owns = jnp.logical_and(mine < chunks, (mine * n) // chunks == me)

    def load(i, src, dst):
        copy = pltpu.make_async_copy(src, dst, in_sem.at[i])
        copy.start()
        return copy

    ins = [
        load(0, g_hbm, g_v),
        load(1, e_hbm, e_v),
        load(2, qt_hbm, qt_v),
        load(3, pr_hbm, pr_v),
        load(4, qr_hbm, qr_v),
        load(5, vg_hbm, vbuf.at[dp]),
        load(6, m_hbm, m_v),
        load(7, vm_hbm, vm_v),
        load(8, w_hbm, w_v),
        load(9, vp_hbm, vp_v),
    ]

    barrier = pltpu.get_barrier_semaphore()
    slot = sc * n_t + tn

    def greet_line(i):
        pl.semaphore_signal(
            barrier, inc=1, device_id=(lax.rem(dp + 1 + i, n_dp), tn, sc), device_id_type=MESH
        )

    def greet_plane(i):
        peer = lax.rem(slot + 1 + i, group)
        pl.semaphore_signal(
            barrier, inc=1, device_id=(dp, lax.rem(peer, n_t), peer // n_t), device_id_type=MESH
        )

    each(n_dp - 1, greet_line)
    each(group - 1, greet_plane)

    ins[2].wait()
    q_hi, q_lo = split(qt_v[...])
    ins[0].wait()
    ins[1].wait()
    merged = g_v[...].astype(F32) + e_v[...]
    e_v[...] = merged
    m_hi, m_lo = split(merged)
    hi_v[...] = m_hi
    lo_v[...] = m_lo
    first = mm(jnp.concatenate([q_hi, q_lo], axis=0), hi_v[...], ((1,), (1,)))
    second = mm(q_hi, lo_v[...], ((1,), (1,)))
    pbuf[dp] = first[:rank] + first[rank:] + second

    pl.semaphore_wait(barrier, n_dp - 1 + group - 1)
    ins[5].wait()

    def send_p(i):
        peer = lax.rem(dp + 1 + i, n_dp)
        pltpu.make_async_remote_copy(
            pbuf.at[dp], pbuf.at[dp], psend, precv, device_id=(peer, tn, sc), device_id_type=MESH
        ).start()

    def send_v(i):
        peer = lax.rem(dp + 1 + i, n_dp)
        pltpu.make_async_remote_copy(
            vbuf.at[dp], vbuf.at[dp], vsend, vrecv, device_id=(peer, tn, sc), device_id_type=MESH
        ).start()

    each(n_dp - 1, send_p)

    ins[3].wait()
    ins[4].wait()
    p_root_left = left_parts(pr_v[...].T)
    q_root_left = left_parts(qr_v[...])

    others = pl.ds(0, n_dp - 1)
    pltpu.make_async_copy(pbuf.at[others], pbuf.at[others], precv).wait()
    if n_dp <= 16:
        p_sum = pbuf[0]
        for i in range(1, n_dp):
            p_sum = p_sum + pbuf[i]
    else:
        p_sum = lax.fori_loop(1, n_dp, lambda i, acc: acc + pbuf[i], pbuf[0])
    pf = mm(p_root_left, right_parts(p_sum))
    pf_hi, pf_lo = split(pf)
    pf_both = jnp.concatenate([pf_hi, pf_lo], axis=0)

    def send_chunk(k):
        owner = (k * n) // chunks
        at = (
            pl.ds((k // col_chunks) * CHUNK_ROWS, CHUNK_ROWS),
            pl.ds((k % col_chunks) * CHUNK_COLS, CHUNK_COLS),
        )

        @pl.when(me == owner)
        def _():
            rbuf[me] = qpart[at]

        @pl.when(me != owner)
        def _():
            pltpu.make_async_remote_copy(
                qpart.at[at], rbuf.at[me], rsend, rrecv,
                device_id=(owner // n_t, owner % n_t, sc), device_id_type=MESH,
            ).start()

    block = 2 * CHUNK_COLS
    for c in range(width // block):
        cols = pl.ds(c * block, block)
        first = mm(pf_both, hi_v[:, cols])
        second = mm(pf_hi, lo_v[:, cols])
        qpart[:, cols] = first[:rank] + first[rank:] + second
        for r in range(rank // CHUNK_ROWS):
            for j in range(2):
                send_chunk(r * col_chunks + 2 * c + j)
    each(n_dp - 1, send_v)

    pf_v[...] = pf
    left = mm(q_root_left, right_parts(pf)).T / n_dp
    left = left_parts(left)

    @pl.when(owns)
    def _():
        whole = pl.ds(0, n - 1)
        pltpu.make_async_copy(rbuf.at[whole], rbuf.at[whole], rrecv).wait()
        if n <= 16:
            q_sum = rbuf[0]
            for i in range(1, n):
                q_sum = q_sum + rbuf[i]
        else:
            q_sum = lax.fori_loop(1, n, lambda i, acc: acc + rbuf[i], rbuf[0])
        qfull[mine] = q_sum

        def send_sum(i):
            peer = lax.rem(2 * n - 1 - me + i, n)

            @pl.when(peer != me)
            def _():
                send_sum_to(peer)

        def send_sum_to(peer):
            pltpu.make_async_remote_copy(
                qfull.at[mine], qfull.at[mine], asend, arecv,
                device_id=(peer // n_t, lax.rem(peer, n_t), sc), device_id_type=MESH,
            ).start()

        each(n, send_sum)
        got = pl.ds(0, chunks - 1)
        pltpu.make_async_copy(qfull.at[got], qfull.at[got], arecv).wait()

    @pl.when(jnp.logical_not(owns))
    def _():
        pltpu.make_async_copy(qfull, qfull, arecv).wait()

    ins[6].wait()
    squares = jnp.zeros((8, 128), F32)
    q_parts = []
    for c in range(width // block):
        cols = pl.ds(c * block, block)
        q_sum = jnp.concatenate(
            [
                jnp.concatenate([qfull[r * col_chunks + 2 * c + j] for j in range(2)], axis=1)
                for r in range(rank // CHUNK_ROWS)
            ],
            axis=0,
        )
        right = right_parts(q_sum)
        q_parts.append(right)
        approx = mm(left, right)
        new = 0.9 * m_v[:, cols] + approx
        mo_v[:, cols] = new
        square = new * new
        for j in range(2):
            squares = squares + jnp.sum(
                square[:, j * 128 : (j + 1) * 128].reshape(rows // 8, 8, 128), axis=0
            )
    pltpu.make_async_copy(vbuf.at[others], vbuf.at[others], vrecv).wait()
    if n_dp <= 16:
        v_sum = vbuf[0]
        for i in range(1, n_dp):
            v_sum = v_sum + vbuf[i]
    else:
        v_sum = lax.fori_loop(1, n_dp, lambda i, acc: acc + vbuf[i], vbuf[0])
    ins[7].wait()
    v_new = 0.9 * vm_v[...] + v_sum / n_dp
    vmo_v[...] = v_new
    v_square = jnp.sum(v_new * v_new)

    corner = jnp.logical_and(
        lax.broadcasted_iota(jnp.int32, (8, 128), 0) == 0,
        lax.broadcasted_iota(jnp.int32, (8, 128), 1) == 0,
    )
    sbuf[slot] = squares + jnp.where(corner, v_square, 0.0)
    for i in range(1, group):
        peer = lax.rem(slot + i, group)
        pltpu.make_async_remote_copy(
            sbuf.at[slot], sbuf.at[slot], ssend, srecv,
            device_id=(dp, lax.rem(peer, n_t), peer // n_t), device_id_type=MESH,
        ).start()
    q_root_t = left_parts(qr_v[...].T)
    for c in range(width // block):
        cols = pl.ds(c * block, block)
        eo_v[:, cols] = e_v[:, cols] - mm(left, q_parts[c])
        qf_v[:, cols] = mm(q_root_t, q_parts[c])
    ins[8].wait()
    ins[9].wait()

    rest = pl.ds(0, group - 1)
    pltpu.make_async_copy(sbuf.at[rest], sbuf.at[rest], srecv).wait()
    total_tile = sbuf[0]
    for i in range(1, group):
        total_tile = total_tile + sbuf[i]
    total = jnp.sum(jnp.sum(total_tile, axis=1, keepdims=True), axis=0, keepdims=True)
    count = n_s * (width * width + 3 * width)
    scale = 0.05 / jnp.sqrt(total / count + 1e-06)
    wo_v[...] = w_v[...] - scale * mo_v[...]
    vpo_v[...] = vp_v[...] - scale.reshape(1, 1, 1) * vmo_v[...]

    pltpu.make_async_copy(pbuf.at[others], pbuf.at[others], psend).wait()
    pltpu.make_async_copy(vbuf.at[others], vbuf.at[others], vsend).wait()
    pltpu.make_async_copy(sbuf.at[rest], sbuf.at[rest], ssend).wait()

    @pl.when(owns)
    def _():
        got = pl.ds(0, chunks - 1)
        pltpu.make_async_copy(qfull.at[got], qfull.at[got], rsend).wait()
        whole = pl.ds(0, n - 1)
        pltpu.make_async_copy(rbuf.at[whole], rbuf.at[whole], asend).wait()

    @pl.when(jnp.logical_not(owns))
    def _():
        pltpu.make_async_copy(qfull, qfull, rsend).wait()


def write(count, *refs):
    sems = refs[2 * count]
    copies = [
        pltpu.make_async_copy(refs[i], refs[count + i], sems.at[i]) for i in range(count)
    ]
    for copy in copies:
        copy.start()
    for copy in copies:
        copy.wait()


def shards(
    sizes,
    grads, errors, q_prev, p_root, q_root, momentum, weights, vec_grads, vec_momentum, vec_params,
):
    n_dp, n_t, n_s = sizes
    rows, width = errors.shape[2:]
    rank = q_prev.shape[2]
    vecs, entries = vec_params.shape[1:]
    n = n_dp * n_t
    chunks = (rank // CHUNK_ROWS) * (width // CHUNK_COLS)
    big = (rows, width)
    vec = (vecs, 1, entries)
    shapes = (big, (rank, rows), (rank, width), big, big, vec, vec)
    any_space = pl.BlockSpec(memory_space=pl.ANY)
    in_vmem = pl.BlockSpec(memory_space=pltpu.VMEM)
    dma = pltpu.SemaphoreType.DMA
    vmem = pltpu.VMEM
    args = (
        grads[0, 0],
        errors[0, 0],
        q_prev[0].T,
        p_root[0],
        q_root[0],
        momentum[0],
        weights[0],
        vec_grads[0, 0][:, None, :],
        vec_momentum[0][:, None, :],
        vec_params[0][:, None, :],
    )
    outs = pl.pallas_call(
        functools.partial(kernel, sizes),
        out_shape=tuple(vmem(shape, F32) for shape in shapes),
        in_specs=[any_space] * 10,
        out_specs=(in_vmem,) * 7,
        scratch_shapes=[
            vmem((rows, width), BF16),
            vmem((rows, width), F32),
            vmem((rank, width), F32),
            vmem((rank, rank), F32),
            vmem((rank, rank), F32),
            vmem((rows, width), F32),
            vmem((rows, width), F32),
            vmem((vecs, 1, entries), F32),
            vmem((vecs, 1, entries), F32),
            vmem((rows, width), BF16),
            vmem((rows, width), BF16),
            vmem((n_dp, rank, rows), F32),
            vmem((n_dp, vecs, 1, entries), F32),
            vmem((rank, width), F32),
            vmem((n, CHUNK_ROWS, CHUNK_COLS), F32),
            vmem((chunks, CHUNK_ROWS, CHUNK_COLS), F32),
            vmem((n_t * n_s, 8, 128), F32),
            dma((10,)),
        ]
        + [dma(())] * 10,
        compiler_params=pltpu.CompilerParams(
            collective_id=0, has_side_effects=True, vmem_limit_bytes=48 * 1024 * 1024
        ),
    )(*(pltpu.with_memory_space_constraint(arg, pltpu.HBM) for arg in args))
    outs = pl.pallas_call(
        functools.partial(write, 7),
        out_shape=tuple(pltpu.HBM(shape, F32) for shape in shapes),
        in_specs=[in_vmem] * 7,
        out_specs=(any_space,) * 7,
        scratch_shapes=[dma((7,))],
    )(*(pltpu.with_memory_space_constraint(out, pltpu.VMEM) for out in outs))
    errors_out, p_factor, q_factor, momentum_out, weights_out, vec_momentum_out, vec_params_out = outs
    return (
        errors_out[None, None],
        p_factor.T[None],
        q_factor.T[None],
        momentum_out[None],
        weights_out[None],
        vec_momentum_out[:, 0][None],
        vec_params_out[:, 0][None],
    )


def solution(mesh):
    sizes = (mesh.shape["dp"], mesh.shape["tensor"], mesh.shape["section"])
    in_specs = (
        P("dp", "section", "tensor", None),
        P("dp", "section", "tensor", None),
        P("section", None, None),
        P("section", None, None),
        P("section", None, None),
        P("section", "tensor", None),
        P("section", "tensor", None),
        P("dp", "section", None, "tensor"),
        P("section", None, "tensor"),
        P("section", None, "tensor"),
    )
    out_specs = (
        P("dp", "section", "tensor", None),
        P("section", "tensor", None),
        P("section", None, None),
        P("section", "tensor", None),
        P("section", "tensor", None),
        P("section", None, "tensor"),
        P("section", None, "tensor"),
    )
    return jax.shard_map(
        functools.partial(shards, sizes),
        mesh=mesh, in_specs=in_specs, out_specs=out_specs, check_vma=False,
    )
```
